512 devices in a mesh: elem: 32 (over y, x), mode: 16 (over z, core).
Axes of the slice: x: 4, y: 8, z: 8, core: 2. Of those that a mesh axis runs over, the one named last changes fastest.
Arguments:
- u_spec: bfloat16 [1024, 65536], P('mode', 'elem'), may hold values from -6 to 6
- dir_spec: bfloat16 [1024, 65536], P('mode', 'elem'), may hold values from -6 to 6
- advecting: bfloat16 [3, 1024, 65536], P(None, None, ('elem', 'mode')), may hold values from -6 to 6
- viscosity: bfloat16 [1024, 65536], P(None, ('elem', 'mode')), may hold values from 0.099609375 to 2
- degrees: int32 [2, 1024], P(None, 'elem'), may hold values from 2 to 7
- edge_side: int32 [4096], P('elem'), may hold values from 0 to 127, as said below
- edge_link: int32 [3, 4096], P(None, 'elem'), may hold values from -1 to 127, as said below
Outputs:
- advect: float32 [1024, 65536], P('mode', 'elem')
- helm_velocity: float32 [1024, 65536], P('mode', 'elem')
- helm_direction: float32 [1024, 65536], P('mode', 'elem')
The draws below stay inside these ranges and needn't reach their ends.
Inputs may be any that keep to these rules, and one draw needn't show every extreme that they name: `edge_side`: within each partition's 128 slots, no element side appears twice. `edge_link`: A slot with peer -1 is empty and has flag 0 and peer slot 0. Pairing is symmetric: a live slot's partner is live, names it back and has the same flag. A peer is the partition itself (another slot) or a partition one or two places away around the closed loop of 32 partitions. At most 24 live slots of one partition name any one other partition as peer, and some partition has exactly that many with each of its four neighbours. Some partition has all 128 slots live.
All inputs are finite; a program needn't handle non-finite values.
Results may differ from the reference program's by a relative error of at most 0.0055.
Values may be sent and summed in bfloat16 or wider, within the bound.
A program may use at most 128 MiB of HBM per device.

```python
import math
import jax
import jax.numpy as jnp
import numpy as np
from jax import lax

Q = 64
NZ = 1024
E_DEV = 32
SLOTS = 128
PARTS_SIZE = 32
E = 1024
ELB = 2


def shuffled_rows(key, row_count, length):
    key_list = jax.random.split(key, row_count)

    def one_row(row_key):
        return jax.random.permutation(row_key, length).astype(jnp.int32)
    return jax.vmap(one_row)(key_list)


def edge_tables(key):
    base_key = jax.random.fold_in(key, 811)
    key_list = jax.random.split(base_key, 10)
    inner_most = SLOTS // 8
    near_most = 3 * SLOTS // 16
    parts_range = jnp.arange(PARTS_SIZE, dtype=jnp.int32)
    busy_part = jax.random.randint(key_list[0], (), 0, PARTS_SIZE)
    inner_pairs = jax.random.randint(key_list[1], (PARTS_SIZE,), 2, inner_most + 1)
    first_pairs = jax.random.randint(key_list[2], (PARTS_SIZE,), 4, near_most + 1)
    second_pairs = jax.random.randint(key_list[3], (PARTS_SIZE,), 4, near_most + 1)
    inner_pairs = jnp.where(parts_range == busy_part, inner_most, inner_pairs)
    first_pairs = jnp.where((parts_range == busy_part) | (parts_range == (busy_part + PARTS_SIZE - 1) % PARTS_SIZE), near_most, first_pairs)
    second_pairs = jnp.where((parts_range == busy_part) | (parts_range == (busy_part + PARTS_SIZE - 2) % PARTS_SIZE), near_most, second_pairs)
    inner_flip = jax.random.randint(key_list[4], (PARTS_SIZE, inner_most), 0, 2)
    first_flip = jax.random.randint(key_list[5], (PARTS_SIZE, near_most), 0, 2)
    second_flip = jax.random.randint(key_list[6], (PARTS_SIZE, near_most), 0, 2)
    owner_part = parts_range[:, None]
    place = jnp.arange(SLOTS, dtype=jnp.int32)[None, :]
    edge_a = 2 * inner_most
    edge_b = edge_a + near_most
    edge_c = edge_b + near_most
    edge_d = edge_c + near_most
    category = (place >= edge_a).astype(jnp.int32) + (place >= edge_b).astype(jnp.int32) + (place >= edge_c).astype(jnp.int32) + (place >= edge_d).astype(jnp.int32)
    category = jnp.broadcast_to(category, (PARTS_SIZE, SLOTS))
    place_full = jnp.broadcast_to(place, (PARTS_SIZE, SLOTS))
    start_of = jnp.where(category == 0, 0, edge_a + (category - 1) * near_most)
    within = place_full - start_of
    pair_index = jnp.where(category == 0, within // 2, within)
    shift_of = jnp.where(category == 0, 0, jnp.where(category == 1, 1, jnp.where(category == 2, -1, jnp.where(category == 3, 2, -2))))
    peer_index = (owner_part + shift_of + PARTS_SIZE) % PARTS_SIZE
    partner_place = jnp.where(category == 0, jnp.bitwise_xor(place_full, 1), jnp.where(category == 1, edge_b + within, jnp.where(category == 2, edge_a + within, jnp.where(category == 3, edge_d + within, edge_c + within))))
    pair_limit = jnp.where(category == 0, inner_pairs[:, None], jnp.where(category == 1, first_pairs[:, None], jnp.where(category == 2, jnp.roll(first_pairs, 1)[:, None], jnp.where(category == 3, second_pairs[:, None], jnp.roll(second_pairs, 2)[:, None]))))
    live_slot = pair_index < pair_limit
    inner_pick = jnp.take_along_axis(inner_flip, jnp.clip(pair_index, 0, inner_most - 1), axis=1)
    near_index = jnp.clip(pair_index, 0, near_most - 1)
    first_pick = jnp.take_along_axis(first_flip, near_index, axis=1)
    first_back = jnp.take_along_axis(jnp.roll(first_flip, 1, axis=0), near_index, axis=1)
    second_pick = jnp.take_along_axis(second_flip, near_index, axis=1)
    second_back = jnp.take_along_axis(jnp.roll(second_flip, 2, axis=0), near_index, axis=1)
    flip_flag = jnp.where(category == 0, inner_pick, jnp.where(category == 1, first_pick, jnp.where(category == 2, first_back, jnp.where(category == 3, second_pick, second_back))))
    slot_of = shuffled_rows(key_list[7], PARTS_SIZE, SLOTS)
    partner_slot = slot_of[peer_index, partner_place]
    inverse = jnp.argsort(slot_of, axis=1)

    def place_slots(values):
        return jnp.take_along_axis(values, inverse, axis=1)
    flip_row = place_slots(jnp.where(live_slot, flip_flag, 0))
    peer_row = place_slots(jnp.where(live_slot, peer_index, -1))
    slot_row = place_slots(jnp.where(live_slot, partner_slot, 0))
    link = jnp.stack([flip_row, peer_row, slot_row], axis=0).reshape(3, PARTS_SIZE * SLOTS).astype(jnp.int32)
    top_value = 4 * E_DEV - 1
    side_order = shuffled_rows(key_list[8], PARTS_SIZE, 4 * E_DEV)
    chosen = jax.random.randint(key_list[9], (PARTS_SIZE,), 0, SLOTS)
    where_top = jnp.argmax((side_order == top_value).astype(jnp.int32), axis=1)
    value_at = jnp.take_along_axis(side_order, chosen[:, None], axis=1)[:, 0]
    row_index = jnp.arange(PARTS_SIZE, dtype=jnp.int32)
    side_order = side_order.at[row_index, where_top].set(value_at)
    side_order = side_order.at[row_index, chosen].set(top_value)
    sides = side_order[:, :SLOTS].reshape(PARTS_SIZE * SLOTS).astype(jnp.int32)
    return (sides, link)


def draw_edge_side(key, part):
    return edge_tables(key)[0]


def draw_edge_link(key, part):
    return edge_tables(key)[1]


def with_ends(drawn, rng, least, high):
    spot = [jax.random.randint(jax.random.fold_in(rng, axis), (), 0, length) for axis, length in enumerate(drawn.shape)]
    longest = drawn.shape.index(max(drawn.shape))
    beside = spot[:longest] + [(spot[longest] + 1) % drawn.shape[longest]] + spot[longest + 1:]
    return drawn.at[tuple(spot)].set(least).at[tuple(beside)].set(high)


def steps_of(key, extent, cuts, smallest, high):
    def one(dim, shards_of):
        draws = jax.random.uniform(jax.random.fold_in(jax.random.fold_in(key, 6), dim), (shards_of,), jnp.float32, smallest / len(cuts), high / len(cuts))
        return jnp.repeat(jnp.exp(draws), extent[dim] // shards_of).reshape((-1,) + (1,) * (len(extent) - dim - 1))

    gain = one(*cuts[0])
    for cut in cuts[1:]:
        gain = gain * one(*cut)
    return gain


def centred(key, extent, spread, limit, pieces=(), kind=jnp.bfloat16):
    drawn = spread * jax.random.normal(key, extent, jnp.float32)
    if pieces:
        drawn = drawn * steps_of(key, extent, pieces, -0.22, 0.18)
    return jnp.clip(drawn, -limit, limit).astype(kind)


def setup_inputs(seed: int = 0) -> dict:
    keys = jax.random.split(jax.random.key(seed), 8)
    u_spec = centred(keys[0], (NZ, E * Q), 1.0, 6.0, ((0, 16), (1, 32)))
    dir_spec = centred(keys[1], (NZ, E * Q), 1.0, 6.0, ((0, 16), (1, 32)))
    advecting = centred(keys[2], (3, NZ, E * Q), 1.0, 6.0, ((2, 512),))
    viscosity = jnp.clip(jnp.exp(math.log(2.0) - 2.9996462 * jax.random.uniform(keys[3], (NZ, E * Q), jnp.float32) ** steps_of(keys[3], (NZ, E * Q), ((1, 512),), -0.2, 0.2)), 0.099609375, 2.0).astype(jnp.bfloat16)
    degrees = with_ends(jax.random.randint(keys[4], (2, E), 2, 8), jax.random.fold_in(keys[4], 1), 2, 7).astype(jnp.int32)
    edge_side = draw_edge_side(jax.random.fold_in(keys[7], 71), 0)
    edge_link = draw_edge_link(jax.random.fold_in(keys[7], 71), 0)
    return {"u_spec": u_spec, "dir_spec": dir_spec, "advecting": advecting, "viscosity": viscosity, "degrees": degrees, "edge_side": edge_side, "edge_link": edge_link}


METRIC = 0.125
AREA_SCALE = 64.0
LENGTH = 8.0
HELM_LAMBDA = 4.0
PENALTY = 0.02

def cheb_tables():
    degree_top = 7
    angles = np.pi * np.arange(degree_top + 1) / degree_top
    cheb_points = np.cos(angles)
    signs_scale = np.ones(degree_top + 1)
    signs_scale[0] = 2.0
    signs_scale[degree_top] = 2.0
    signs_scale = signs_scale * (-1.0) ** np.arange(degree_top + 1)
    differences = cheb_points[:, None] - cheb_points[None, :]
    derivative = signs_scale[:, None] / signs_scale[None, :] / (differences + np.eye(degree_top + 1))
    derivative = derivative - np.eye(degree_top + 1) * derivative.sum(axis=1)[:, None]
    weights = np.zeros(degree_top + 1)
    interior = np.ones(degree_top - 1)
    for k in range(1, (degree_top - 1) // 2 + 1):
        interior = interior - 2.0 * np.cos(2 * k * angles[1:degree_top]) / (4 * k * k - 1)
    weights[0] = 1.0 / (degree_top * degree_top)
    weights[degree_top] = weights[0]
    weights[1:degree_top] = 2.0 * interior / degree_top
    return (derivative, weights)

def node_tables():
    derivative, weights = cheb_tables()
    identity_eight = np.eye(8)
    node_x = np.kron(METRIC * derivative, identity_eight)
    node_y = np.kron(identity_eight, METRIC * derivative)
    mass = AREA_SCALE * np.outer(weights, weights).reshape(-1)
    edge_weight = LENGTH * weights
    return (jnp.asarray(node_x, dtype=jnp.float32), jnp.asarray(node_y, dtype=jnp.float32), jnp.asarray(mass, dtype=jnp.float32), jnp.asarray(edge_weight, dtype=jnp.float32))

def synthesis_table(total_count):
    planes = jnp.arange(total_count, dtype=jnp.int32)
    wave_index = planes // 2
    turn_count = planes[:, None] * wave_index[None, :] % total_count
    angles = 2.0 * math.pi / total_count * turn_count.astype(jnp.float32)
    level_scale = math.sqrt(2.0 / total_count)
    parity = (planes % 2)[None, :]
    synthesis = jnp.where(parity == 0, jnp.cos(angles), jnp.sin(angles)) * level_scale
    alternating = (1 - 2 * (planes % 2)).astype(jnp.float32)[:, None] / math.sqrt(total_count)
    column = planes[None, :]
    synthesis = jnp.where(column == 0, jnp.float32(1.0 / math.sqrt(total_count)), synthesis)
    synthesis = jnp.where(column == 1, alternating, synthesis)
    return synthesis.astype(jnp.bfloat16)

def z_derivative(coeffs):
    total_count = coeffs.shape[-2]
    paired = coeffs.reshape(coeffs.shape[:-2] + (total_count // 2, 2, coeffs.shape[-1]))
    rate_table = (4.0 / total_count * jnp.arange(total_count // 2, dtype=jnp.float32))[:, None]
    even_part = rate_table * paired[..., 1, :]
    odd_part = -rate_table * paired[..., 0, :]
    return jnp.stack([even_part, odd_part], axis=-2).reshape(coeffs.shape)

def side_nodes(side_code, position):
    return jnp.where(side_code == 0, position, jnp.where(side_code == 1, 8 * position + 7, jnp.where(side_code == 2, 63 - position, 8 * (7 - position))))

def reference(u_spec, dir_spec, advecting, viscosity, degrees, edge_side, edge_link):
    node_x, node_y, mass, edge_weight = node_tables()
    synthesis = synthesis_table(NZ)
    block_width = Q * ELB
    columns = jnp.arange(E * Q, dtype=jnp.int32)
    mass_columns = mass[columns % block_width // ELB]
    velocity = advecting.astype(jnp.float32)
    weighted = mass_columns[None, :] * viscosity.astype(jnp.float32)

    def node_apply(field_data, matrix):
        shaped = field_data.reshape(NZ, E // ELB, Q, ELB)
        result = jnp.einsum('pq,zbql->zbpl', matrix, shaped, precision=lax.Precision.HIGHEST)
        return result.reshape(NZ, E * Q)

    def gradients(spec_field):
        slope_hat = z_derivative(spec_field.astype(jnp.float32)).astype(jnp.bfloat16)
        plain_phys = jnp.dot(synthesis, spec_field, preferred_element_type=jnp.float32)
        along_z = jnp.dot(synthesis, slope_hat, preferred_element_type=jnp.float32)
        return (node_apply(plain_phys, node_x), node_apply(plain_phys, node_y), along_z)

    def volume(gradient_set):
        grad_x, grad_y, along_z = gradient_set
        flat_sum = node_apply(weighted * grad_x, node_x.T) + node_apply(weighted * grad_y, node_y.T)
        co_flat = jnp.dot(synthesis.T, flat_sum.astype(jnp.bfloat16), preferred_element_type=jnp.float32)
        co_span = jnp.dot(synthesis.T, (weighted * along_z).astype(jnp.bfloat16), preferred_element_type=jnp.float32)
        return co_flat - z_derivative(co_span)
    flip_flag = edge_link[0]
    peer_part = edge_link[1]
    peer_slot = edge_link[2]
    slots_all = PARTS_SIZE * SLOTS
    owner_part = jnp.arange(slots_all, dtype=jnp.int32) // SLOTS
    element = owner_part * E_DEV + edge_side // 4
    side_code = edge_side % 4
    position = jnp.arange(8, dtype=jnp.int32)
    side_node = side_nodes(side_code[:, None], position[None, :])
    slot_columns = ((element // ELB)[:, None] * block_width + side_node * ELB + (element % ELB)[:, None]).reshape(-1)
    live_slot = peer_part >= 0
    safe_peer = jnp.maximum(peer_part, 0)
    source = safe_peer * SLOTS + peer_slot
    turned = jnp.where(flip_flag[:, None] == 1, 7 - position[None, :], position[None, :])
    partner = (source[:, None] * 8 + turned).reshape(-1)
    normal_degree = jnp.where(side_code % 2 == 0, degrees[0][element], degrees[1][element]).astype(jnp.float32)
    joint_degree = jnp.maximum(normal_degree, normal_degree[source])
    strength = jnp.where(live_slot, PENALTY * (joint_degree + 1.0) * (joint_degree + 1.0), jnp.float32(0.0))
    factor = (strength[:, None] * edge_weight[None, :]).reshape(-1)

    def penalty(spec_field):
        traces = spec_field[:, slot_columns].astype(jnp.float32)
        others = traces[:, partner]
        penalty_terms = factor[None, :] * (traces - others)
        return jnp.zeros((NZ, E * Q), jnp.float32).at[:, slot_columns].add(penalty_terms)
    grads_velocity = gradients(u_spec)
    moved_phys = (velocity[0] * grads_velocity[0] + velocity[1] * grads_velocity[1] + velocity[2] * grads_velocity[2]).astype(jnp.bfloat16)
    advect = jnp.dot(synthesis.T, moved_phys, preferred_element_type=jnp.float32)
    helm_velocity = HELM_LAMBDA * mass_columns[None, :] * u_spec.astype(jnp.float32) + volume(grads_velocity) + penalty(u_spec)
    helm_direction = HELM_LAMBDA * mass_columns[None, :] * dir_spec.astype(jnp.float32) + volume(gradients(dir_spec)) + penalty(dir_spec)
    return (advect, helm_velocity, helm_direction)
```

```python
import math

import jax
import jax.numpy as jnp
import ml_dtypes
import numpy as np
from jax import lax
from jax.experimental import pallas as pl
from jax.experimental.pallas import tpu as pltpu
from jax.sharding import PartitionSpec as P

METRIC = 0.125
AREA_SCALE = 64.0
LENGTH = 8.0
HELM_LAMBDA = 4.0
PENALTY = 0.02
OFFSETS = (1, 2, -1, -2)
NEAR = 24
LANES = 128
F32 = jnp.float32
BF16 = jnp.bfloat16


def cheb_tables():
    top = 7
    angles = np.pi * np.arange(top + 1) / top
    points = np.cos(angles)
    scale = np.ones(top + 1)
    scale[0] = 2.0
    scale[top] = 2.0
    scale = scale * (-1.0) ** np.arange(top + 1)
    differences = points[:, None] - points[None, :]
    derivative = scale[:, None] / scale[None, :] / (differences + np.eye(top + 1))
    derivative = derivative - np.eye(top + 1) * derivative.sum(axis=1)[:, None]
    weights = np.zeros(top + 1)
    interior = np.ones(top - 1)
    for k in range(1, (top - 1) // 2 + 1):
        interior = interior - 2.0 * np.cos(2 * k * angles[1:top]) / (4 * k * k - 1)
    weights[0] = 1.0 / (top * top)
    weights[top] = weights[0]
    weights[1:top] = 2.0 * interior / top
    return derivative, weights


def synthesis_table(total):
    planes = np.arange(total)
    turns = planes[:, None] * (planes // 2)[None, :] % total
    angles = 2.0 * np.pi / total * turns
    table = np.where((planes % 2)[None, :] == 0, np.cos(angles), np.sin(angles))
    table = table * math.sqrt(2.0 / total)
    table[:, 0] = 1.0 / math.sqrt(total)
    table[:, 1] = (1 - 2 * (planes % 2)) / math.sqrt(total)
    return table.astype(np.float32).astype(ml_dtypes.bfloat16)


def operator_tables(block_elements):
    derivative, weights = cheb_tables()
    eye8 = np.eye(8)
    eye_block = np.eye(block_elements)
    kron_x = np.kron(np.kron(METRIC * derivative, eye8), eye_block).astype(np.float32)
    kron_y = np.kron(np.kron(eye8, METRIC * derivative), eye_block).astype(np.float32)

    def halves(matrix):
        high = matrix.astype(ml_dtypes.bfloat16)
        low = (matrix - high.astype(np.float32)).astype(ml_dtypes.bfloat16)
        return np.concatenate([high, high, low], axis=0)

    forward = halves(np.concatenate([kron_x.T, kron_y.T], axis=1))
    backward = halves(np.concatenate([kron_x, kron_y], axis=0))
    mass = np.repeat(AREA_SCALE * np.outer(weights, weights).reshape(-1), block_elements)
    return forward, backward, mass.astype(np.float32)[None, :]


def split_dot(values, stacked):
    high = values.astype(BF16)
    low = (values - high.astype(F32)).astype(BF16)
    return jnp.dot(
        jnp.concatenate([high, low, high], axis=1), stacked, preferred_element_type=F32
    )


def span_slope(values, first_row, total):
    rows = values.shape[0]
    row = lax.broadcasted_iota(jnp.int32, values.shape, 0)
    rate = (4.0 / total) * ((row + first_row) >> 1).astype(F32)
    above = pltpu.roll(values, rows - 1, 0)
    below = pltpu.roll(values, 1, 0)
    return rate * jnp.where((row & 1) == 0, above, -below)


def planes_kernel(
    coeff_ref, adv_ref, visc_ref, syn_ref, fwd_ref, bwd_ref, mass_ref, out_ref, stack, back
):
    blocks, _, rows, width = coeff_ref.shape
    total = blocks * rows
    for b in range(blocks):
        for f in range(2):
            values = coeff_ref[b, f]
            span = pl.ds(b * rows, rows)
            stack[span, pl.ds(2 * f * width, width)] = values
            stack[span, pl.ds((2 * f + 1) * width, width)] = span_slope(
                values.astype(F32), b * rows, total
            ).astype(BF16)
    chunk = 256
    for c in range(total // chunk):
        span = pl.ds(c * chunk, chunk)
        phys = jnp.dot(syn_ref[span, :], stack[...], preferred_element_type=F32)
        weighted = mass_ref[...] * visc_ref[span, :].astype(F32)
        for f in range(2):
            plain = phys[:, 2 * f * width : (2 * f + 1) * width]
            along = phys[:, (2 * f + 1) * width : (2 * f + 2) * width]
            grads = split_dot(plain, fwd_ref[...])
            grad_x = grads[:, :width]
            grad_y = grads[:, width:]
            if f == 0:
                moved = (
                    adv_ref[0, span, :].astype(F32) * grad_x
                    + adv_ref[1, span, :].astype(F32) * grad_y
                    + adv_ref[2, span, :].astype(F32) * along
                )
                back[span, pl.ds(0, width)] = moved.astype(BF16)
            flat = split_dot(
                jnp.concatenate([weighted * grad_x, weighted * grad_y], axis=1), bwd_ref[...]
            )
            back[span, pl.ds((2 * f + 1) * width, width)] = flat.astype(BF16)
            back[span, pl.ds((2 * f + 2) * width, width)] = (weighted * along).astype(BF16)
    for c in range(total // chunk):
        spec = lax.dot_general(
            syn_ref[:, pl.ds(c * chunk, chunk)],
            back[...],
            (((0,), (0,)), ((), ())),
            preferred_element_type=F32,
        )
        for f in range(3):
            part = spec[:, :width]
            if f > 0:
                low = (2 * f - 1) * width
                part = spec[:, low : low + width] - span_slope(
                    spec[:, low + width : low + 2 * width], c * chunk, total
                )
            part = part.astype(BF16)
            for b in range(chunk // rows):
                out_ref[c * (chunk // rows) + b, f] = part[b * rows : (b + 1) * rows]


def split_kernel(u_ref, d_ref, out_ref):
    width = out_ref.shape[3]
    for b in range(out_ref.shape[0]):
        span = pl.ds(b * width, width)
        out_ref[b, 0] = u_ref[:, span]
        out_ref[b, 1] = d_ref[:, span]


class SlotTables:
    def __init__(self, deg_ref, side_ref, link_ref):
        slots = side_ref.shape[1]
        self.slots = slots
        self.sub = lax.broadcasted_iota(jnp.int32, (slots, slots), 0)
        self.lane = lax.broadcasted_iota(jnp.int32, (slots, slots), 1)
        self.eye = self.sub == self.lane
        side = side_ref[...]
        element = side >> 2
        code = side & 3
        start = jnp.where(code == 0, 0, jnp.where(code == 1, 7, jnp.where(code == 2, 63, 56)))
        step = jnp.where(code == 0, 1, jnp.where(code == 1, 8, jnp.where(code == 2, -1, -8)))
        first = (element >> 1) * LANES + (element & 1) + 2 * start
        self.first_row = first.astype(F32)
        self.step_row = (2 * step).astype(F32)
        self.flip_row = link_ref[0:1, :].astype(F32)
        self.peer_row = link_ref[1:2, :].astype(F32)
        self.slot_row = link_ref[2:3, :].astype(F32)
        element_col = self.column(element.astype(F32))
        code_col = self.column((code & 1).astype(F32))
        count = deg_ref.shape[1]
        member = lax.broadcasted_iota(jnp.int32, (slots, count), 1).astype(F32) == element_col
        degree = jnp.where(
            code_col == 0.0, deg_ref[0:1, :].astype(F32), deg_ref[1:2, :].astype(F32)
        )
        self.degree_col = jnp.sum(jnp.where(member, degree, 0.0), axis=1, keepdims=True)
        self.degree_row = jnp.sum(
            jnp.where(self.eye, self.degree_col, 0.0), axis=0, keepdims=True
        )
        self.peer_col = self.column(self.peer_row)

    def column(self, row):
        return jnp.sum(jnp.where(self.eye, row, 0.0), axis=1, keepdims=True)

    def peer_of(self, offset):
        parts = lax.axis_size("elem")
        return ((lax.axis_index("elem") + offset + parts) % parts).astype(F32)

    def chosen(self, offset, before):
        peer = self.peer_of(offset)
        ahead = jnp.where((self.peer_col == peer) & before, 1.0, 0.0)
        place = jnp.sum(ahead, axis=0, keepdims=True)
        order = lax.broadcasted_iota(jnp.int32, (NEAR, self.slots), 0).astype(F32)
        return jnp.where((self.peer_row == peer) & (place == order), 1.0, 0.0)


def trace_kernel(u_ref, d_ref, deg_ref, side_ref, link_ref, trace_ref, packed_ref):
    tables = SlotTables(deg_ref, side_ref, link_ref)
    columns = u_ref.shape[1]
    values = jnp.concatenate([u_ref[...], d_ref[...]], axis=0)
    before = tables.sub < tables.lane
    picks = [tables.chosen(offset, before) for offset in OFFSETS]
    picks_all = jnp.concatenate(picks, axis=0).astype(BF16)
    first_col = tables.column(tables.first_row)
    step_col = tables.column(tables.step_row)
    ids = lax.broadcasted_iota(jnp.int32, (tables.slots, columns), 1)
    nt = (((1,), (1,)), ((), ()))
    for k in range(8):
        wanted = (first_col + step_col * float(k)).astype(jnp.int32)
        hot = jnp.where(ids == wanted, 1.0, 0.0).astype(BF16)
        trace = lax.dot_general(values, hot, nt, preferred_element_type=F32).astype(BF16)
        trace_ref[k] = trace
        packed = lax.dot_general(picks_all, trace, nt, preferred_element_type=F32)
        for o in range(4):
            packed_ref[o, k] = packed[o * NEAR : (o + 1) * NEAR].astype(BF16)
    for o in range(4):
        degree = jnp.sum(picks[o] * tables.degree_row, axis=1, keepdims=True)
        packed_ref[o, 8] = jnp.broadcast_to(degree, (NEAR, LANES)).astype(BF16)


def penalty_kernel(
    edge_weight,
    u_ref,
    d_ref,
    deg_ref,
    side_ref,
    link_ref,
    mass_ref,
    trace_ref,
    near0,
    near1,
    near2,
    near3,
    out_ref,
    left,
):
    nears = (near0, near1, near2, near3)
    tables = SlotTables(deg_ref, side_ref, link_ref)
    rows, columns = u_ref.shape
    slot_col = tables.column(tables.slot_row)

    def aims(match, other_degree):
        def pick(row):
            return jnp.sum(match * row, axis=1, keepdims=True)

        alive = pick(jnp.ones_like(tables.degree_row))
        return alive, pick(tables.first_row), pick(tables.step_row), pick(
            tables.degree_row
        ), other_degree

    mine = tables.peer_of(0)
    match = jnp.where(
        (tables.peer_col == mine) & (slot_col == tables.lane.astype(F32)), 1.0, 0.0
    )
    flips = [tables.column(tables.flip_row)]
    sets = [aims(match, tables.degree_col)]
    before = slot_col < tables.slot_row
    for o, offset in enumerate(OFFSETS):
        match = tables.chosen(offset, before)
        flips.append(jnp.sum(match * tables.flip_row, axis=1, keepdims=True))
        sets.append(aims(match, nears[o][8].astype(F32)[:, 0:1]))
    filler = 2 * LANES - tables.slots - 4 * NEAR
    zeros = jnp.zeros((filler, 1), F32)

    def joined(parts):
        return jnp.concatenate(list(parts) + [zeros], axis=0)

    alive = joined(s[0] for s in sets)
    first = joined(s[1] for s in sets)
    step = joined(s[2] for s in sets)
    degree = jnp.maximum(joined(s[3] for s in sets), joined(s[4] for s in sets))
    flip = joined(flips)
    first = jnp.where(alive > 0.0, first + 7.0 * flip * step, -1.0e6)
    step = step * (1.0 - 2.0 * flip)
    strength = alive * PENALTY * (degree + 1.0) * (degree + 1.0)
    for k in range(8):
        received = jnp.concatenate(
            [near[k].astype(F32) for near in nears] + [jnp.zeros((filler, LANES), F32)], axis=0
        )
        left[pl.ds(0, LANES), pl.ds(k * 2 * LANES, LANES)] = trace_ref[k]
        left[pl.ds(0, LANES), pl.ds((k * 2 + 1) * LANES, LANES)] = received.T.astype(BF16)
    left[pl.ds(LANES, 16), :] = jnp.ones((16, left.shape[1]), BF16)
    wide = 256
    ids = lax.broadcasted_iota(jnp.int32, (2 * LANES, wide), 1)
    targets = [(first + step * float(k)).astype(jnp.int32) for k in range(8)]
    factors = [strength * float(edge_weight[k]) for k in range(8)]
    mass = HELM_LAMBDA * jnp.concatenate([mass_ref[...]] * (wide // LANES), axis=1)
    for c in range(columns // wide):
        hot = jnp.concatenate(
            [
                jnp.where(ids == targets[k] - c * wide, factors[k], 0.0).astype(BF16)
                for k in range(8)
            ],
            axis=0,
        )
        summed = jnp.dot(left[...], hot, preferred_element_type=F32)
        scale = mass + summed[LANES : LANES + 1, :]
        span = pl.ds(c * wide, wide)
        out_ref[0, :, span] = scale * u_ref[:, span].astype(F32) - summed[:rows]
        out_ref[1, :, span] = scale * d_ref[:, span].astype(F32) - summed[rows : 2 * rows]


def final_kernel(back_ref, local_ref, adv_ref, vel_ref, dir_ref):
    width = back_ref.shape[3]
    for b in range(back_ref.shape[0]):
        span = pl.ds(b * width, width)
        adv_ref[:, span] = back_ref[b, 0].astype(F32)
        vel_ref[:, span] = local_ref[0, :, span] + back_ref[b, 1].astype(F32)
        dir_ref[:, span] = local_ref[1, :, span] + back_ref[b, 2].astype(F32)


def call(kernel, outs, name, scratch=(), cost=None):
    return pl.pallas_call(
        kernel,
        out_shape=outs,
        scratch_shapes=list(scratch),
        name=name,
        cost_estimate=cost,
        compiler_params=pltpu.CompilerParams(vmem_limit_bytes=48 * 1024 * 1024),
    )


def cost(flops, moved):
    return pl.CostEstimate(flops=flops, bytes_accessed=moved, transcendentals=0)


def on_device(u_spec, dir_spec, advecting, viscosity, degrees, edge_side, edge_link):
    shape = jax.ShapeDtypeStruct
    modes = lax.axis_size("mode")
    total, width = viscosity.shape
    rows, columns = u_spec.shape
    forward, backward, mass = operator_tables(degrees.shape[1] // modes)
    weights = LENGTH * cheb_tables()[1]
    side = edge_side[None, :]
    slots = edge_side.shape[0]

    sent = call(split_kernel, shape((modes, 2, rows, width), BF16), "split")(u_spec, dir_spec)
    coeffs = lax.all_to_all(sent, "mode", split_axis=0, concat_axis=0, tiled=True)

    traces, packed = call(
        trace_kernel,
        (shape((8, 2 * rows, slots), BF16), shape((4, 9, NEAR, LANES), BF16)),
        "trace",
        cost=cost(1 << 29, 1 << 20),
    )(u_spec, dir_spec, degrees, side, edge_link)
    parts = lax.axis_size("elem")
    nears = [
        lax.ppermute(packed[o], "elem", [((i + offset) % parts, i) for i in range(parts)])
        for o, offset in enumerate((-d for d in OFFSETS))
    ]
    nears = [nears[2], nears[3], nears[0], nears[1]]
    local = call(
        lambda *refs: penalty_kernel(weights, *refs),
        shape((2, rows, columns), F32),
        "penalty",
        scratch=[pltpu.VMEM((LANES + 16, 16 * LANES), BF16)],
        cost=cost(1 << 30, 1 << 21),
    )(u_spec, dir_spec, degrees, side, edge_link, mass, traces, *nears)

    returned = call(
        planes_kernel,
        shape((modes, 3, rows, width), BF16),
        "planes",
        scratch=[pltpu.VMEM((total, 4 * width), BF16), pltpu.VMEM((total, 5 * width), BF16)],
        cost=cost(1 << 32, 1 << 22),
    )(coeffs, advecting, viscosity, synthesis_table(total), forward, backward, mass)
    volumes = lax.all_to_all(returned, "mode", split_axis=0, concat_axis=0, tiled=True)
    out = shape((rows, columns), F32)
    return call(final_kernel, (out, out, out), "final")(volumes, local)


def solution(mesh):
    in_specs = (
        P("mode", "elem"),
        P("mode", "elem"),
        P(None, None, ("elem", "mode")),
        P(None, ("elem", "mode")),
        P(None, "elem"),
        P("elem"),
        P(None, "elem"),
    )
    out_specs = (P("mode", "elem"), P("mode", "elem"), P("mode", "elem"))
    return jax.shard_map(
        on_device, mesh=mesh, in_specs=in_specs, out_specs=out_specs, check_vma=False
    )
```

```python
import math

import jax
import jax.numpy as jnp
import ml_dtypes
import numpy as np
from jax import lax
from jax.experimental import pallas as pl
from jax.experimental.pallas import tpu as pltpu
from jax.sharding import PartitionSpec as P

METRIC = 0.125
AREA_SCALE = 64.0
LENGTH = 8.0
HELM_LAMBDA = 4.0
PENALTY = 0.02
OFFSETS = (1, 2, -1, -2)
NEAR = 24
LANES = 128
F32 = jnp.float32
BF16 = jnp.bfloat16


def cheb_tables():
    top = 7
    angles = np.pi * np.arange(top + 1) / top
    points = np.cos(angles)
    scale = np.ones(top + 1)
    scale[0] = 2.0
    scale[top] = 2.0
    scale = scale * (-1.0) ** np.arange(top + 1)
    differences = points[:, None] - points[None, :]
    derivative = scale[:, None] / scale[None, :] / (differences + np.eye(top + 1))
    derivative = derivative - np.eye(top + 1) * derivative.sum(axis=1)[:, None]
    weights = np.zeros(top + 1)
    interior = np.ones(top - 1)
    for k in range(1, (top - 1) // 2 + 1):
        interior = interior - 2.0 * np.cos(2 * k * angles[1:top]) / (4 * k * k - 1)
    weights[0] = 1.0 / (top * top)
    weights[top] = weights[0]
    weights[1:top] = 2.0 * interior / top
    return derivative, weights


def synthesis_table(total):
    planes = np.arange(total)
    turns = planes[:, None] * (planes // 2)[None, :] % total
    angles = 2.0 * np.pi / total * turns
    table = np.where((planes % 2)[None, :] == 0, np.cos(angles), np.sin(angles))
    table = table * math.sqrt(2.0 / total)
    table[:, 0] = 1.0 / math.sqrt(total)
    table[:, 1] = (1 - 2 * (planes % 2)) / math.sqrt(total)
    return table.astype(np.float32).astype(ml_dtypes.bfloat16)


def operator_tables(block_elements):
    derivative, weights = cheb_tables()
    eye8 = np.eye(8)
    eye_block = np.eye(block_elements)
    kron_x = np.kron(np.kron(METRIC * derivative, eye8), eye_block).astype(np.float32)
    kron_y = np.kron(np.kron(eye8, METRIC * derivative), eye_block).astype(np.float32)

    def halves(matrix):
        high = matrix.astype(ml_dtypes.bfloat16)
        low = (matrix - high.astype(np.float32)).astype(ml_dtypes.bfloat16)
        return np.concatenate([high, high, low], axis=0)

    forward = halves(np.concatenate([kron_x.T, kron_y.T], axis=1))
    backward = halves(np.concatenate([kron_x, kron_y], axis=0))
    mass = np.repeat(AREA_SCALE * np.outer(weights, weights).reshape(-1), block_elements)
    return forward, backward, mass.astype(np.float32)[None, :]


def split_dot(values, stacked):
    high = values.astype(BF16)
    low = (values - high.astype(F32)).astype(BF16)
    return jnp.dot(
        jnp.concatenate([high, low, high], axis=1), stacked, preferred_element_type=F32
    )


def span_slope(values, first_row, total):
    rows = values.shape[0]
    row = lax.broadcasted_iota(jnp.int32, values.shape, 0)
    rate = (4.0 / total) * ((row + first_row) >> 1).astype(F32)
    above = pltpu.roll(values, rows - 1, 0)
    below = pltpu.roll(values, 1, 0)
    return rate * jnp.where((row & 1) == 0, above, -below)


def field_planes(field, adv_ref, visc_ref, syn_ref, fwd_ref, bwd_ref, mass_ref, stack, back, out_ref):
    modes, _, rows, width = out_ref.shape
    total = modes * rows
    for b in range(modes):
        span = pl.ds(b * rows, rows)
        stack[field, span, pl.ds(width, width)] = span_slope(
            stack[field, span, pl.ds(0, width)].astype(F32), b * rows, total
        ).astype(BF16)
    chunk = 256
    lead = 1 if field == 0 else 0
    for c in range(total // chunk):
        span = pl.ds(c * chunk, chunk)
        phys = jnp.dot(syn_ref[span, :], stack[field], preferred_element_type=F32)
        weighted = mass_ref[...] * visc_ref[span, :].astype(F32)
        along = phys[:, width:]
        grads = split_dot(phys[:, :width], fwd_ref[...])
        grad_x = grads[:, :width]
        grad_y = grads[:, width:]
        if field == 0:
            moved = (
                adv_ref[0, span, :].astype(F32) * grad_x
                + adv_ref[1, span, :].astype(F32) * grad_y
                + adv_ref[2, span, :].astype(F32) * along
            )
            back[span, pl.ds(2 * width, width)] = moved.astype(BF16)
        flat = split_dot(
            jnp.concatenate([weighted * grad_x, weighted * grad_y], axis=1), bwd_ref[...]
        )
        back[span, pl.ds(0, width)] = flat.astype(BF16)
        back[span, pl.ds(width, width)] = (weighted * along).astype(BF16)
    for c in range(total // chunk):
        spec = lax.dot_general(
            syn_ref[:, pl.ds(c * chunk, chunk)],
            back[:, pl.ds(0, (2 + lead) * width)],
            (((0,), (0,)), ((), ())),
            preferred_element_type=F32,
        )
        parts = [
            spec[:, :width] - span_slope(spec[:, width : 2 * width], c * chunk, total)
        ]
        if field == 0:
            parts.append(spec[:, 2 * width :])
        for i, part in enumerate(parts):
            part = part.astype(BF16)
            for b in range(chunk // rows):
                out_ref[c * (chunk // rows) + b, i] = part[b * rows : (b + 1) * rows]


class SlotTables:
    def __init__(self, deg_ref, side_ref, link_ref):
        slots = side_ref.shape[1]
        self.slots = slots
        self.sub = lax.broadcasted_iota(jnp.int32, (slots, slots), 0)
        self.lane = lax.broadcasted_iota(jnp.int32, (slots, slots), 1)
        self.eye = self.sub == self.lane
        side = side_ref[...]
        element = side >> 2
        code = side & 3
        start = jnp.where(code == 0, 0, jnp.where(code == 1, 7, jnp.where(code == 2, 63, 56)))
        step = jnp.where(code == 0, 1, jnp.where(code == 1, 8, jnp.where(code == 2, -1, -8)))
        first = (element >> 1) * LANES + (element & 1) + 2 * start
        self.first_row = first.astype(F32)
        self.step_row = (2 * step).astype(F32)
        self.flip_row = link_ref[0:1, :].astype(F32)
        self.peer_row = link_ref[1:2, :].astype(F32)
        self.slot_row = link_ref[2:3, :].astype(F32)
        element_col = self.column(element.astype(F32))
        code_col = self.column((code & 1).astype(F32))
        count = deg_ref.shape[1]
        member = lax.broadcasted_iota(jnp.int32, (slots, count), 1).astype(F32) == element_col
        degree = jnp.where(
            code_col == 0.0, deg_ref[0:1, :].astype(F32), deg_ref[1:2, :].astype(F32)
        )
        self.degree_col = jnp.sum(jnp.where(member, degree, 0.0), axis=1, keepdims=True)
        self.degree_row = jnp.sum(
            jnp.where(self.eye, self.degree_col, 0.0), axis=0, keepdims=True
        )
        self.peer_col = self.column(self.peer_row)

    def column(self, row):
        return jnp.sum(jnp.where(self.eye, row, 0.0), axis=1, keepdims=True)

    def peer_of(self, offset):
        parts = lax.axis_size("elem")
        return ((lax.axis_index("elem") + offset + parts) % parts).astype(F32)

    def chosen(self, offset, before):
        peer = self.peer_of(offset)
        ahead = jnp.where((self.peer_col == peer) & before, 1.0, 0.0)
        place = jnp.sum(ahead, axis=0, keepdims=True)
        order = lax.broadcasted_iota(jnp.int32, (NEAR, self.slots), 0).astype(F32)
        return jnp.where((self.peer_row == peer) & (place == order), 1.0, 0.0)


def send_traces(tables, u_ref, d_ref, left, packed_ref):
    columns = u_ref.shape[1]
    values = jnp.concatenate([u_ref[...], d_ref[...]], axis=0)
    before = tables.sub < tables.lane
    picks = [tables.chosen(offset, before) for offset in OFFSETS]
    picks_all = jnp.concatenate(picks, axis=0).astype(BF16)
    first_col = tables.column(tables.first_row)
    step_col = tables.column(tables.step_row)
    ids = lax.broadcasted_iota(jnp.int32, (tables.slots, columns), 1)
    nt = (((1,), (1,)), ((), ()))
    for k in range(8):
        wanted = (first_col + step_col * float(k)).astype(jnp.int32)
        hot = jnp.where(ids == wanted, 1.0, 0.0).astype(BF16)
        trace = lax.dot_general(values, hot, nt, preferred_element_type=F32).astype(BF16)
        left[pl.ds(0, LANES), pl.ds(k * 2 * LANES, LANES)] = trace
        packed = lax.dot_general(picks_all, trace, nt, preferred_element_type=F32)
        for o in range(4):
            packed_ref[o, k] = packed[o * NEAR : (o + 1) * NEAR].astype(BF16)
    for o in range(4):
        degree = jnp.sum(picks[o] * tables.degree_row, axis=1, keepdims=True)
        packed_ref[o, 8] = jnp.broadcast_to(degree, (NEAR, LANES)).astype(BF16)


def local_terms(edge_weight, tables, u_ref, d_ref, mass_ref, nears, left, vel_ref, dir_ref):
    rows, columns = u_ref.shape
    slot_col = tables.column(tables.slot_row)

    def aims(match, other_degree):
        def pick(row):
            return jnp.sum(match * row, axis=1, keepdims=True)

        alive = pick(jnp.ones_like(tables.degree_row))
        return alive, pick(tables.first_row), pick(tables.step_row), pick(
            tables.degree_row
        ), other_degree

    mine = tables.peer_of(0)
    match = jnp.where(
        (tables.peer_col == mine) & (slot_col == tables.lane.astype(F32)), 1.0, 0.0
    )
    flips = [tables.column(tables.flip_row)]
    sets = [aims(match, tables.degree_col)]
    before = slot_col < tables.slot_row
    for o, offset in enumerate(OFFSETS):
        match = tables.chosen(offset, before)
        flips.append(jnp.sum(match * tables.flip_row, axis=1, keepdims=True))
        sets.append(aims(match, nears[o, 8].astype(F32)[:, 0:1]))
    filler = 2 * LANES - tables.slots - 4 * NEAR
    zeros = jnp.zeros((filler, 1), F32)

    def joined(parts):
        return jnp.concatenate(list(parts) + [zeros], axis=0)

    alive = joined(s[0] for s in sets)
    first = joined(s[1] for s in sets)
    step = joined(s[2] for s in sets)
    degree = jnp.maximum(joined(s[3] for s in sets), joined(s[4] for s in sets))
    flip = joined(flips)
    first = jnp.where(alive > 0.0, first + 7.0 * flip * step, -1.0e6)
    step = step * (1.0 - 2.0 * flip)
    strength = alive * PENALTY * (degree + 1.0) * (degree + 1.0)
    for k in range(8):
        received = jnp.concatenate(
            [nears[o, k].astype(F32) for o in range(4)] + [jnp.zeros((filler, LANES), F32)],
            axis=0,
        )
        left[pl.ds(0, LANES), pl.ds((k * 2 + 1) * LANES, LANES)] = received.T.astype(BF16)
    left[pl.ds(LANES, 16), :] = jnp.ones((16, left.shape[1]), BF16)
    wide = 256
    ids = lax.broadcasted_iota(jnp.int32, (2 * LANES, wide), 1)
    targets = [(first + step * float(k)).astype(jnp.int32) for k in range(8)]
    factors = [strength * float(edge_weight[k]) for k in range(8)]
    mass = HELM_LAMBDA * jnp.concatenate([mass_ref[...]] * (wide // LANES), axis=1)
    for c in range(columns // wide):
        hot = jnp.concatenate(
            [
                jnp.where(ids == targets[k] - c * wide, factors[k], 0.0).astype(BF16)
                for k in range(8)
            ],
            axis=0,
        )
        summed = jnp.dot(left[...], hot, preferred_element_type=F32)
        scale = mass + summed[LANES : LANES + 1, :]
        span = pl.ds(c * wide, wide)
        vel_ref[:, span] = scale * u_ref[:, span].astype(F32) - summed[:rows]
        dir_ref[:, span] = scale * d_ref[:, span].astype(F32) - summed[rows : 2 * rows]


ROUTES = [(dz, dc) for dz in (4, 3, 5, 2, 6, 1, 7, 0) for dc in (0, 1) if (dz, dc) != (0, 0)]


def whole_kernel(
    edge_weight,
    u_ref,
    d_ref,
    adv_hbm,
    visc_hbm,
    deg_ref,
    side_ref,
    link_ref,
    syn_hbm,
    fwd_ref,
    bwd_ref,
    mass_ref,
    adv_out,
    vel_out,
    dir_out,
    adv_ref,
    visc_ref,
    syn_ref,
    stack,
    back,
    ret_u,
    ret_d,
    got_u,
    got_d,
    left,
    packed,
    nears,
    load_sem,
    in_send,
    in_recv,
    u_send,
    u_recv,
    d_send,
    d_recv,
    halo_send,
    halo_recv,
):
    elem = lax.axis_index("elem")
    mode = lax.axis_index("mode")
    parts = lax.axis_size("elem")
    chips = lax.axis_size("mode") // 2
    chip = lax.div(mode, 2)
    core = lax.rem(mode, 2)
    rows = u_ref.shape[0]
    width = visc_ref.shape[1]
    modes_to = [
        lax.rem(chip + dz, chips) * 2 + lax.rem(core + dc, 2) for dz, dc in ROUTES
    ]
    elems_to = [lax.rem(elem + offset + parts, parts) for offset in OFFSETS]
    mesh_ids = pl.DeviceIdType.MESH

    barrier = pltpu.get_barrier_semaphore()
    for other in modes_to:
        pl.semaphore_signal(barrier, inc=1, device_id=(elem, other), device_id_type=mesh_ids)
    for other in elems_to:
        pl.semaphore_signal(barrier, inc=1, device_id=(other, mode), device_id_type=mesh_ids)
    loads = [
        pltpu.make_async_copy(syn_hbm, syn_ref, load_sem.at[0]),
        pltpu.make_async_copy(visc_hbm, visc_ref, load_sem.at[1]),
        pltpu.make_async_copy(adv_hbm, adv_ref, load_sem.at[2]),
    ]
    for load in loads:
        load.start()
    pl.semaphore_wait(barrier, len(modes_to) + len(elems_to))

    my_rows = pl.ds(pl.multiple_of(mode * rows, rows), rows)
    incoming = []
    for f, source in enumerate((u_ref, d_ref)):
        copies = []
        for j, other in enumerate(modes_to):
            copy = pltpu.make_async_remote_copy(
                src_ref=source.at[:, pl.ds(pl.multiple_of(other * width, width), width)],
                dst_ref=stack.at[f, my_rows, pl.ds(0, width)],
                send_sem=in_send.at[f, j],
                recv_sem=in_recv.at[f, j],
                device_id=(elem, other),
                device_id_type=mesh_ids,
            )
            copy.start()
            copies.append(copy)
        incoming.append(copies)
    tables = SlotTables(deg_ref, side_ref, link_ref)
    send_traces(tables, u_ref, d_ref, left, packed)
    halo = []
    for o, other in enumerate(elems_to):
        copy = pltpu.make_async_remote_copy(
            src_ref=packed.at[o],
            dst_ref=nears.at[(o + 2) % 4],
            send_sem=halo_send.at[o],
            recv_sem=halo_recv.at[o],
            device_id=(other, mode),
            device_id_type=mesh_ids,
        )
        copy.start()
        halo.append(copy)
    for f, source in enumerate((u_ref, d_ref)):
        stack[f, my_rows, pl.ds(0, width)] = source[
            :, pl.ds(pl.multiple_of(mode * width, width), width)
        ]
    for load in loads:
        load.wait()
    outgoing = []
    for f, (ret, got, send, recv) in enumerate(
        ((ret_u, got_u, u_send, u_recv), (ret_d, got_d, d_send, d_recv))
    ):
        for copy in incoming[f]:
            copy.wait_recv()
        field_planes(
            f, adv_ref, visc_ref, syn_ref, fwd_ref, bwd_ref, mass_ref, stack, back, ret
        )
        copies = []
        for j, other in enumerate(modes_to):
            copy = pltpu.make_async_remote_copy(
                src_ref=ret.at[other],
                dst_ref=got.at[mode],
                send_sem=send.at[j],
                recv_sem=recv.at[j],
                device_id=(elem, other),
                device_id_type=mesh_ids,
            )
            copy.start()
            copies.append(copy)
        got[mode] = ret[mode]
        outgoing.append(copies)
    for copy in halo:
        copy.wait_recv()
    local_terms(edge_weight, tables, u_ref, d_ref, mass_ref, nears, left, vel_out, dir_out)
    for copy in outgoing[0]:
        copy.wait_recv()
    for b in range(got_u.shape[0]):
        span = pl.ds(b * width, width)
        vel_out[:, span] += got_u[b, 0].astype(F32)
        adv_out[:, span] = got_u[b, 1].astype(F32)
    for copy in outgoing[1]:
        copy.wait_recv()
    for b in range(got_d.shape[0]):
        span = pl.ds(b * width, width)
        dir_out[:, span] += got_d[b, 0].astype(F32)
    for copy in incoming[0] + incoming[1] + halo + outgoing[0] + outgoing[1]:
        copy.wait_send()


def on_device(u_spec, dir_spec, advecting, viscosity, degrees, edge_side, edge_link):
    modes = lax.axis_size("mode")
    total, width = viscosity.shape
    rows, columns = u_spec.shape
    forward, backward, mass = operator_tables(degrees.shape[1] // modes)
    weights = LENGTH * cheb_tables()[1]
    out = jax.ShapeDtypeStruct((rows, columns), F32)
    near = pl.BlockSpec(memory_space=pltpu.VMEM)
    far = pl.BlockSpec(memory_space=pltpu.HBM)
    routes = len(ROUTES)
    return pl.pallas_call(
        lambda *refs: whole_kernel(weights, *refs),
        out_shape=(out, out, out),
        in_specs=[near, near, far, far, near, near, near, far, near, near, near],
        out_specs=(near, near, near),
        scratch_shapes=[
            pltpu.VMEM((3, total, width), BF16),
            pltpu.VMEM((total, width), BF16),
            pltpu.VMEM((total, total), BF16),
            pltpu.VMEM((2, total, 2 * width), BF16),
            pltpu.VMEM((total, 3 * width), BF16),
            pltpu.VMEM((modes, 2, rows, width), BF16),
            pltpu.VMEM((modes, 1, rows, width), BF16),
            pltpu.VMEM((modes, 2, rows, width), BF16),
            pltpu.VMEM((modes, 1, rows, width), BF16),
            pltpu.VMEM((LANES + 16, 16 * LANES), BF16),
            pltpu.VMEM((4, 9, NEAR, LANES), BF16),
            pltpu.VMEM((4, 9, NEAR, LANES), BF16),
            pltpu.SemaphoreType.DMA((3,)),
            pltpu.SemaphoreType.DMA((2, routes)),
            pltpu.SemaphoreType.DMA((2, routes)),
            pltpu.SemaphoreType.DMA((routes,)),
            pltpu.SemaphoreType.DMA((routes,)),
            pltpu.SemaphoreType.DMA((routes,)),
            pltpu.SemaphoreType.DMA((routes,)),
            pltpu.SemaphoreType.DMA((4,)),
            pltpu.SemaphoreType.DMA((4,)),
        ],
        name="whole",
        compiler_params=pltpu.CompilerParams(
            collective_id=0, has_side_effects=True, vmem_limit_bytes=48 * 1024 * 1024
        ),
    )(
        u_spec,
        dir_spec,
        advecting,
        viscosity,
        degrees,
        edge_side[None, :],
        edge_link,
        synthesis_table(total),
        forward,
        backward,
        mass,
    )


def solution(mesh):
    in_specs = (
        P("mode", "elem"),
        P("mode", "elem"),
        P(None, None, ("elem", "mode")),
        P(None, ("elem", "mode")),
        P(None, "elem"),
        P("elem"),
        P(None, "elem"),
    )
    out_specs = (P("mode", "elem"), P("mode", "elem"), P("mode", "elem"))
    return jax.shard_map(
        on_device, mesh=mesh, in_specs=in_specs, out_specs=out_specs, check_vma=False
    )
```

```python
import math

import jax
import jax.numpy as jnp
import ml_dtypes
import numpy as np
from jax import lax
from jax.experimental import pallas as pl
from jax.experimental.pallas import tpu as pltpu
from jax.sharding import PartitionSpec as P

METRIC = 0.125
AREA_SCALE = 64.0
LENGTH = 8.0
HELM_LAMBDA = 4.0
PENALTY = 0.02
OFFSETS = (1, 2, -1, -2)
NEAR = 24
LANES = 128
F32 = jnp.float32
BF16 = jnp.bfloat16


def cheb_tables():
    top = 7
    angles = np.pi * np.arange(top + 1) / top
    points = np.cos(angles)
    scale = np.ones(top + 1)
    scale[0] = 2.0
    scale[top] = 2.0
    scale = scale * (-1.0) ** np.arange(top + 1)
    differences = points[:, None] - points[None, :]
    derivative = scale[:, None] / scale[None, :] / (differences + np.eye(top + 1))
    derivative = derivative - np.eye(top + 1) * derivative.sum(axis=1)[:, None]
    weights = np.zeros(top + 1)
    interior = np.ones(top - 1)
    for k in range(1, (top - 1) // 2 + 1):
        interior = interior - 2.0 * np.cos(2 * k * angles[1:top]) / (4 * k * k - 1)
    weights[0] = 1.0 / (top * top)
    weights[top] = weights[0]
    weights[1:top] = 2.0 * interior / top
    return derivative, weights


def synthesis_table(total):
    planes = np.arange(total)
    turns = planes[:, None] * (planes // 2)[None, :] % total
    angles = 2.0 * np.pi / total * turns
    table = np.where((planes % 2)[None, :] == 0, np.cos(angles), np.sin(angles))
    table = table * math.sqrt(2.0 / total)
    table[:, 0] = 1.0 / math.sqrt(total)
    table[:, 1] = (1 - 2 * (planes % 2)) / math.sqrt(total)
    return table.astype(np.float32).astype(ml_dtypes.bfloat16)


def operator_tables(block_elements):
    derivative, weights = cheb_tables()
    eye8 = np.eye(8)
    eye_block = np.eye(block_elements)
    kron_x = np.kron(np.kron(METRIC * derivative, eye8), eye_block).astype(np.float32)
    kron_y = np.kron(np.kron(eye8, METRIC * derivative), eye_block).astype(np.float32)

    def halves(matrix):
        high = matrix.astype(ml_dtypes.bfloat16)
        low = (matrix - high.astype(np.float32)).astype(ml_dtypes.bfloat16)
        return np.concatenate([high, high, low], axis=0)

    forward = halves(np.concatenate([kron_x.T, kron_y.T], axis=1))
    backward = halves(np.concatenate([kron_x, kron_y], axis=0))
    mass = np.repeat(AREA_SCALE * np.outer(weights, weights).reshape(-1), block_elements)
    return forward, backward, mass.astype(np.float32)[None, :]


def split_dot(values, stacked):
    high = values.astype(BF16)
    low = (values - high.astype(F32)).astype(BF16)
    return jnp.dot(
        jnp.concatenate([high, low, high], axis=1), stacked, preferred_element_type=F32
    )


def span_slope(values, first_row, total):
    rows = values.shape[0]
    row = lax.broadcasted_iota(jnp.int32, values.shape, 0)
    rate = (4.0 / total) * ((row + first_row) >> 1).astype(F32)
    above = pltpu.roll(values, rows - 1, 0)
    below = pltpu.roll(values, 1, 0)
    return rate * jnp.where((row & 1) == 0, above, -below)


def field_planes(field, adv_ref, visc_ref, syn_ref, fwd_ref, bwd_ref, mass_ref, stack, back, out_ref):
    modes, _, rows, width = out_ref.shape
    total = modes * rows
    for b in range(modes):
        span = pl.ds(b * rows, rows)
        stack[field, span, pl.ds(width, width)] = span_slope(
            stack[field, span, pl.ds(0, width)].astype(F32), b * rows, total
        ).astype(BF16)
    chunk = 256
    lead = 1 if field == 0 else 0
    for c in range(total // chunk):
        span = pl.ds(c * chunk, chunk)
        phys = jnp.dot(syn_ref[span, :], stack[field], preferred_element_type=F32)
        weighted = mass_ref[...] * visc_ref[span, :].astype(F32)
        along = phys[:, width:]
        grads = split_dot(phys[:, :width], fwd_ref[...])
        grad_x = grads[:, :width]
        grad_y = grads[:, width:]
        if field == 0:
            moved = (
                adv_ref[0, span, :].astype(F32) * grad_x
                + adv_ref[1, span, :].astype(F32) * grad_y
                + adv_ref[2, span, :].astype(F32) * along
            )
            back[span, pl.ds(2 * width, width)] = moved.astype(BF16)
        flat = split_dot(
            jnp.concatenate([weighted * grad_x, weighted * grad_y], axis=1), bwd_ref[...]
        )
        back[span, pl.ds(0, width)] = flat.astype(BF16)
        back[span, pl.ds(width, width)] = (weighted * along).astype(BF16)
    for c in range(total // chunk):
        spec = lax.dot_general(
            syn_ref[:, pl.ds(c * chunk, chunk)],
            back[:, pl.ds(0, (2 + lead) * width)],
            (((0,), (0,)), ((), ())),
            preferred_element_type=F32,
        )
        parts = [
            spec[:, :width] - span_slope(spec[:, width : 2 * width], c * chunk, total)
        ]
        if field == 0:
            parts.append(spec[:, 2 * width :])
        for i, part in enumerate(parts):
            part = part.astype(BF16)
            for b in range(chunk // rows):
                out_ref[c * (chunk // rows) + b, i] = part[b * rows : (b + 1) * rows]


class SlotTables:
    def __init__(self, deg_ref, side_ref, link_ref):
        slots = side_ref.shape[1]
        self.slots = slots
        self.sub = lax.broadcasted_iota(jnp.int32, (slots, slots), 0)
        self.lane = lax.broadcasted_iota(jnp.int32, (slots, slots), 1)
        self.eye = self.sub == self.lane
        side = side_ref[...]
        element = side >> 2
        code = side & 3
        start = jnp.where(code == 0, 0, jnp.where(code == 1, 7, jnp.where(code == 2, 63, 56)))
        step = jnp.where(code == 0, 1, jnp.where(code == 1, 8, jnp.where(code == 2, -1, -8)))
        first = (element >> 1) * LANES + (element & 1) + 2 * start
        self.first_row = first.astype(F32)
        self.step_row = (2 * step).astype(F32)
        self.flip_row = link_ref[0:1, :].astype(F32)
        self.peer_row = link_ref[1:2, :].astype(F32)
        self.slot_row = link_ref[2:3, :].astype(F32)
        element_col = self.column(element.astype(F32))
        code_col = self.column((code & 1).astype(F32))
        count = deg_ref.shape[1]
        member = lax.broadcasted_iota(jnp.int32, (slots, count), 1).astype(F32) == element_col
        degree = jnp.where(
            code_col == 0.0, deg_ref[0:1, :].astype(F32), deg_ref[1:2, :].astype(F32)
        )
        self.degree_col = jnp.sum(jnp.where(member, degree, 0.0), axis=1, keepdims=True)
        self.degree_row = jnp.sum(
            jnp.where(self.eye, self.degree_col, 0.0), axis=0, keepdims=True
        )
        self.peer_col = self.column(self.peer_row)

    def column(self, row):
        return jnp.sum(jnp.where(self.eye, row, 0.0), axis=1, keepdims=True)

    def peer_of(self, offset):
        parts = lax.axis_size("elem")
        return ((lax.axis_index("elem") + offset + parts) % parts).astype(F32)

    def chosen(self, offset, before):
        peer = self.peer_of(offset)
        ahead = jnp.where((self.peer_col == peer) & before, 1.0, 0.0)
        place = jnp.sum(ahead, axis=0, keepdims=True)
        order = lax.broadcasted_iota(jnp.int32, (NEAR, self.slots), 0).astype(F32)
        return jnp.where((self.peer_row == peer) & (place == order), 1.0, 0.0)


def send_traces(tables, u_ref, d_ref, left, packed_ref):
    columns = u_ref.shape[1]
    values = jnp.concatenate([u_ref[...], d_ref[...]], axis=0)
    before = tables.sub < tables.lane
    picks = [tables.chosen(offset, before) for offset in OFFSETS]
    picks_all = jnp.concatenate(picks, axis=0).astype(BF16)
    first_col = tables.column(tables.first_row)
    step_col = tables.column(tables.step_row)
    ids = lax.broadcasted_iota(jnp.int32, (tables.slots, columns), 1)
    nt = (((1,), (1,)), ((), ()))
    for k in range(8):
        wanted = (first_col + step_col * float(k)).astype(jnp.int32)
        hot = jnp.where(ids == wanted, 1.0, 0.0).astype(BF16)
        trace = lax.dot_general(values, hot, nt, preferred_element_type=F32).astype(BF16)
        left[pl.ds(0, LANES), pl.ds(k * 2 * LANES, LANES)] = trace
        packed = lax.dot_general(picks_all, trace, nt, preferred_element_type=F32)
        for o in range(4):
            packed_ref[o, k] = packed[o * NEAR : (o + 1) * NEAR].astype(BF16)
    for o in range(4):
        degree = jnp.sum(picks[o] * tables.degree_row, axis=1, keepdims=True)
        packed_ref[o, 8] = jnp.broadcast_to(degree, (NEAR, LANES)).astype(BF16)


def local_terms(edge_weight, tables, u_ref, d_ref, mass_ref, nears, left, vel_ref, dir_ref):
    rows, columns = u_ref.shape
    slot_col = tables.column(tables.slot_row)

    def aims(match, other_degree):
        def pick(row):
            return jnp.sum(match * row, axis=1, keepdims=True)

        alive = pick(jnp.ones_like(tables.degree_row))
        return alive, pick(tables.first_row), pick(tables.step_row), pick(
            tables.degree_row
        ), other_degree

    mine = tables.peer_of(0)
    match = jnp.where(
        (tables.peer_col == mine) & (slot_col == tables.lane.astype(F32)), 1.0, 0.0
    )
    flips = [tables.column(tables.flip_row)]
    sets = [aims(match, tables.degree_col)]
    before = slot_col < tables.slot_row
    for o, offset in enumerate(OFFSETS):
        match = tables.chosen(offset, before)
        flips.append(jnp.sum(match * tables.flip_row, axis=1, keepdims=True))
        sets.append(aims(match, nears[o, 8].astype(F32)[:, 0:1]))
    filler = 2 * LANES - tables.slots - 4 * NEAR
    zeros = jnp.zeros((filler, 1), F32)

    def joined(parts):
        return jnp.concatenate(list(parts) + [zeros], axis=0)

    alive = joined(s[0] for s in sets)
    first = joined(s[1] for s in sets)
    step = joined(s[2] for s in sets)
    degree = jnp.maximum(joined(s[3] for s in sets), joined(s[4] for s in sets))
    flip = joined(flips)
    first = jnp.where(alive > 0.0, first + 7.0 * flip * step, -1.0e6)
    step = step * (1.0 - 2.0 * flip)
    strength = alive * PENALTY * (degree + 1.0) * (degree + 1.0)
    for k in range(8):
        received = jnp.concatenate(
            [nears[o, k].astype(F32) for o in range(4)] + [jnp.zeros((filler, LANES), F32)],
            axis=0,
        )
        left[pl.ds(0, LANES), pl.ds((k * 2 + 1) * LANES, LANES)] = received.T.astype(BF16)
    left[pl.ds(LANES, 16), :] = jnp.ones((16, left.shape[1]), BF16)
    wide = 256
    ids = lax.broadcasted_iota(jnp.int32, (2 * LANES, wide), 1)
    targets = [(first + step * float(k)).astype(jnp.int32) for k in range(8)]
    factors = [strength * float(edge_weight[k]) for k in range(8)]
    mass = HELM_LAMBDA * jnp.concatenate([mass_ref[...]] * (wide // LANES), axis=1)
    for c in range(columns // wide):
        hot = jnp.concatenate(
            [
                jnp.where(ids == targets[k] - c * wide, factors[k], 0.0).astype(BF16)
                for k in range(8)
            ],
            axis=0,
        )
        summed = jnp.dot(left[...], hot, preferred_element_type=F32)
        scale = mass + summed[LANES : LANES + 1, :]
        span = pl.ds(c * wide, wide)
        vel_ref[:, span] = scale * u_ref[:, span].astype(F32) - summed[:rows]
        dir_ref[:, span] = scale * d_ref[:, span].astype(F32) - summed[rows : 2 * rows]


ROUTES = [(dz, dc) for dz in (4, 3, 5, 2, 6, 1, 7, 0) for dc in (0, 1) if (dz, dc) != (0, 0)]


def whole_kernel(
    edge_weight,
    u_hbm,
    d_hbm,
    adv_hbm,
    visc_hbm,
    syn_hbm,
    fwd_hbm,
    bwd_hbm,
    mass_hbm,
    deg_ref,
    side_ref,
    link_ref,
    got_u,
    got_d,
    local_hbm,
    u_ref,
    d_ref,
    adv_ref,
    visc_ref,
    syn_ref,
    fwd_ref,
    bwd_ref,
    mass_ref,
    local,
    stack,
    back,
    ret_u,
    ret_d,
    left,
    packed,
    nears,
    load_sem,
    in_send,
    in_recv,
    u_send,
    u_recv,
    d_send,
    d_recv,
    halo_send,
    halo_recv,
):
    elem = lax.axis_index("elem")
    mode = lax.axis_index("mode")
    parts = lax.axis_size("elem")
    chips = lax.axis_size("mode") // 2
    chip = lax.div(mode, 2)
    core = lax.rem(mode, 2)
    rows = u_ref.shape[0]
    width = visc_ref.shape[1]
    modes_to = [
        lax.rem(chip + dz, chips) * 2 + lax.rem(core + dc, 2) for dz, dc in ROUTES
    ]
    elems_to = [lax.rem(elem + offset + parts, parts) for offset in OFFSETS]
    mesh_ids = pl.DeviceIdType.MESH

    barrier = pltpu.get_barrier_semaphore()
    for other in modes_to:
        pl.semaphore_signal(barrier, inc=1, device_id=(elem, other), device_id_type=mesh_ids)
    for other in elems_to:
        pl.semaphore_signal(barrier, inc=1, device_id=(other, mode), device_id_type=mesh_ids)
    pairs = (
        (u_hbm, u_ref),
        (d_hbm, d_ref),
        (syn_hbm, syn_ref),
        (fwd_hbm, fwd_ref),
        (bwd_hbm, bwd_ref),
        (mass_hbm, mass_ref),
        (visc_hbm, visc_ref),
        (adv_hbm, adv_ref),
    )
    loads = [
        pltpu.make_async_copy(source, target, load_sem.at[i])
        for i, (source, target) in enumerate(pairs)
    ]
    for load in loads:
        load.start()
    pl.semaphore_wait(barrier, len(modes_to) + len(elems_to))

    my_rows = pl.ds(pl.multiple_of(mode * rows, rows), rows)
    incoming = []
    for f, source in enumerate((u_hbm, d_hbm)):
        copies = []
        for j, other in enumerate(modes_to):
            copy = pltpu.make_async_remote_copy(
                src_ref=source.at[:, pl.ds(pl.multiple_of(other * width, width), width)],
                dst_ref=stack.at[f, my_rows, pl.ds(0, width)],
                send_sem=in_send.at[f, j],
                recv_sem=in_recv.at[f, j],
                device_id=(elem, other),
                device_id_type=mesh_ids,
            )
            copy.start()
            copies.append(copy)
        incoming.append(copies)
    tables = SlotTables(deg_ref, side_ref, link_ref)
    for load in loads[:2]:
        load.wait()
    send_traces(tables, u_ref, d_ref, left, packed)
    halo = []
    for o, other in enumerate(elems_to):
        copy = pltpu.make_async_remote_copy(
            src_ref=packed.at[o],
            dst_ref=nears.at[(o + 2) % 4],
            send_sem=halo_send.at[o],
            recv_sem=halo_recv.at[o],
            device_id=(other, mode),
            device_id_type=mesh_ids,
        )
        copy.start()
        halo.append(copy)
    for f, source in enumerate((u_ref, d_ref)):
        stack[f, my_rows, pl.ds(0, width)] = source[
            :, pl.ds(pl.multiple_of(mode * width, width), width)
        ]
    for load in loads[2:]:
        load.wait()
    outgoing = []
    stores = []
    for f, (ret, got, send, recv) in enumerate(
        ((ret_u, got_u, u_send, u_recv), (ret_d, got_d, d_send, d_recv))
    ):
        for copy in incoming[f]:
            copy.wait_recv()
        field_planes(
            f, adv_ref, visc_ref, syn_ref, fwd_ref, bwd_ref, mass_ref, stack, back, ret
        )
        copies = []
        for j, other in enumerate(modes_to):
            copy = pltpu.make_async_remote_copy(
                src_ref=ret.at[other],
                dst_ref=got.at[mode],
                send_sem=send.at[j],
                recv_sem=recv.at[j],
                device_id=(elem, other),
                device_id_type=mesh_ids,
            )
            copy.start()
            copies.append(copy)
        store = pltpu.make_async_copy(ret.at[mode], got.at[mode], load_sem.at[8 + f])
        store.start()
        stores.append(store)
        outgoing.append(copies)
    for copy in halo:
        copy.wait_recv()
    local_terms(
        edge_weight, tables, u_ref, d_ref, mass_ref, nears, left, local.at[0], local.at[1]
    )
    store = pltpu.make_async_copy(local, local_hbm, load_sem.at[10])
    store.start()
    stores.append(store)
    for copy in outgoing[0] + outgoing[1]:
        copy.wait_recv()
    for store in stores:
        store.wait()
    for copy in incoming[0] + incoming[1] + halo + outgoing[0] + outgoing[1]:
        copy.wait_send()


def final_kernel(got_u, got_d, local, adv_out, vel_out, dir_out):
    width = got_u.shape[3]
    for b in range(got_u.shape[0]):
        span = pl.ds(b * width, width)
        vel_out[:, span] = local[0, :, span] + got_u[b, 0].astype(F32)
        adv_out[:, span] = got_u[b, 1].astype(F32)
        dir_out[:, span] = local[1, :, span] + got_d[b, 0].astype(F32)


VMEM_BYTES = 67043328


def on_device(u_spec, dir_spec, advecting, viscosity, degrees, edge_side, edge_link):
    modes = lax.axis_size("mode")
    total, width = viscosity.shape
    rows, columns = u_spec.shape
    forward, backward, mass = operator_tables(degrees.shape[1] // modes)
    weights = LENGTH * cheb_tables()[1]
    shape = jax.ShapeDtypeStruct
    near = pl.BlockSpec(memory_space=pltpu.VMEM)
    far = pl.BlockSpec(memory_space=pltpu.HBM)
    routes = len(ROUTES)
    got_u, got_d, local = pl.pallas_call(
        lambda *refs: whole_kernel(weights, *refs),
        out_shape=(
            shape((modes, 2, rows, width), BF16),
            shape((modes, 1, rows, width), BF16),
            shape((2, rows, columns), F32),
        ),
        in_specs=[far] * 8 + [near] * 3,
        out_specs=(far, far, far),
        scratch_shapes=[
            pltpu.VMEM((rows, columns), BF16),
            pltpu.VMEM((rows, columns), BF16),
            pltpu.VMEM((3, total, width), BF16),
            pltpu.VMEM((total, width), BF16),
            pltpu.VMEM((total, total), BF16),
            pltpu.VMEM(forward.shape, BF16),
            pltpu.VMEM(backward.shape, BF16),
            pltpu.VMEM(mass.shape, F32),
            pltpu.VMEM((2, rows, columns), F32),
            pltpu.VMEM((2, total, 2 * width), BF16),
            pltpu.VMEM((total, 3 * width), BF16),
            pltpu.VMEM((modes, 2, rows, width), BF16),
            pltpu.VMEM((modes, 1, rows, width), BF16),
            pltpu.VMEM((LANES + 16, 16 * LANES), BF16),
            pltpu.VMEM((4, 9, NEAR, LANES), BF16),
            pltpu.VMEM((4, 9, NEAR, LANES), BF16),
            pltpu.SemaphoreType.DMA((11,)),
            pltpu.SemaphoreType.DMA((2, routes)),
            pltpu.SemaphoreType.DMA((2, routes)),
            pltpu.SemaphoreType.DMA((routes,)),
            pltpu.SemaphoreType.DMA((routes,)),
            pltpu.SemaphoreType.DMA((routes,)),
            pltpu.SemaphoreType.DMA((routes,)),
            pltpu.SemaphoreType.DMA((4,)),
            pltpu.SemaphoreType.DMA((4,)),
        ],
        name="whole",
        compiler_params=pltpu.CompilerParams(
            collective_id=0, has_side_effects=True, vmem_limit_bytes=VMEM_BYTES
        ),
    )(
        u_spec,
        dir_spec,
        advecting,
        viscosity,
        synthesis_table(total),
        forward,
        backward,
        mass,
        degrees,
        edge_side[None, :],
        edge_link,
    )
    out = shape((rows, columns), F32)
    return pl.pallas_call(
        final_kernel,
        out_shape=(out, out, out),
        name="final",
        compiler_params=pltpu.CompilerParams(vmem_limit_bytes=VMEM_BYTES),
    )(got_u, got_d, local)


def solution(mesh):
    in_specs = (
        P("mode", "elem"),
        P("mode", "elem"),
        P(None, None, ("elem", "mode")),
        P(None, ("elem", "mode")),
        P(None, "elem"),
        P("elem"),
        P(None, "elem"),
    )
    out_specs = (P("mode", "elem"), P("mode", "elem"), P("mode", "elem"))
    return jax.shard_map(
        on_device, mesh=mesh, in_specs=in_specs, out_specs=out_specs, check_vma=False
    )
```

```python
import math

import jax
import jax.numpy as jnp
import ml_dtypes
import numpy as np
from jax import lax
from jax.experimental import pallas as pl
from jax.experimental.pallas import tpu as pltpu
from jax.sharding import PartitionSpec as P

METRIC = 0.125
AREA_SCALE = 64.0
LENGTH = 8.0
HELM_LAMBDA = 4.0
PENALTY = 0.02
OFFSETS = (1, 2, -1, -2)
NEAR = 24
LANES = 128
F32 = jnp.float32
BF16 = jnp.bfloat16


def cheb_tables():
    top = 7
    angles = np.pi * np.arange(top + 1) / top
    points = np.cos(angles)
    scale = np.ones(top + 1)
    scale[0] = 2.0
    scale[top] = 2.0
    scale = scale * (-1.0) ** np.arange(top + 1)
    differences = points[:, None] - points[None, :]
    derivative = scale[:, None] / scale[None, :] / (differences + np.eye(top + 1))
    derivative = derivative - np.eye(top + 1) * derivative.sum(axis=1)[:, None]
    weights = np.zeros(top + 1)
    interior = np.ones(top - 1)
    for k in range(1, (top - 1) // 2 + 1):
        interior = interior - 2.0 * np.cos(2 * k * angles[1:top]) / (4 * k * k - 1)
    weights[0] = 1.0 / (top * top)
    weights[top] = weights[0]
    weights[1:top] = 2.0 * interior / top
    return derivative, weights


def synthesis_table(total):
    planes = np.arange(total)
    turns = planes[:, None] * (planes // 2)[None, :] % total
    angles = 2.0 * np.pi / total * turns
    table = np.where((planes % 2)[None, :] == 0, np.cos(angles), np.sin(angles))
    table = table * math.sqrt(2.0 / total)
    table[:, 0] = 1.0 / math.sqrt(total)
    table[:, 1] = (1 - 2 * (planes % 2)) / math.sqrt(total)
    return table.astype(np.float32).astype(ml_dtypes.bfloat16)


def operator_tables(block_elements):
    derivative, weights = cheb_tables()
    eye8 = np.eye(8)
    eye_block = np.eye(block_elements)
    kron_x = np.kron(np.kron(METRIC * derivative, eye8), eye_block).astype(np.float32)
    kron_y = np.kron(np.kron(eye8, METRIC * derivative), eye_block).astype(np.float32)

    def halves(matrix):
        high = matrix.astype(ml_dtypes.bfloat16)
        low = (matrix - high.astype(np.float32)).astype(ml_dtypes.bfloat16)
        return np.concatenate([high, high, low], axis=0)

    forward = halves(np.concatenate([kron_x.T, kron_y.T], axis=1))
    backward = halves(np.concatenate([kron_x, kron_y], axis=0))
    mass = np.repeat(AREA_SCALE * np.outer(weights, weights).reshape(-1), block_elements)
    return forward, backward, mass.astype(np.float32)[None, :]


def split_dot(values, stacked):
    high = values.astype(BF16)
    low = (values - high.astype(F32)).astype(BF16)
    return jnp.dot(
        jnp.concatenate([high, low, high], axis=1), stacked, preferred_element_type=F32
    )


def span_slope(values, first_row, total):
    rows = values.shape[0]
    row = lax.broadcasted_iota(jnp.int32, values.shape, 0)
    rate = (4.0 / total) * ((row + first_row) >> 1).astype(F32)
    above = pltpu.roll(values, rows - 1, 0)
    below = pltpu.roll(values, 1, 0)
    return rate * jnp.where((row & 1) == 0, above, -below)


def field_planes(field, adv_ref, visc_ref, syn_ref, fwd_ref, bwd_ref, mass_ref, stack, back, out_ref):
    modes, _, rows, width = out_ref.shape
    total = modes * rows
    for b in range(modes):
        span = pl.ds(b * rows, rows)
        stack[field, span, pl.ds(width, width)] = span_slope(
            stack[field, span, pl.ds(0, width)].astype(F32), b * rows, total
        ).astype(BF16)
    chunk = 256
    lead = 1 if field == 0 else 0
    for c in range(total // chunk):
        span = pl.ds(c * chunk, chunk)
        phys = jnp.dot(syn_ref[span, :], stack[field], preferred_element_type=F32)
        weighted = mass_ref[...] * visc_ref[span, :].astype(F32)
        along = phys[:, width:]
        grads = split_dot(phys[:, :width], fwd_ref[...])
        grad_x = grads[:, :width]
        grad_y = grads[:, width:]
        if field == 0:
            moved = (
                adv_ref[0, span, :].astype(F32) * grad_x
                + adv_ref[1, span, :].astype(F32) * grad_y
                + adv_ref[2, span, :].astype(F32) * along
            )
            back[span, pl.ds(2 * width, width)] = moved.astype(BF16)
        flat = split_dot(
            jnp.concatenate([weighted * grad_x, weighted * grad_y], axis=1), bwd_ref[...]
        )
        back[span, pl.ds(0, width)] = flat.astype(BF16)
        back[span, pl.ds(width, width)] = (weighted * along).astype(BF16)
    for c in range(total // chunk):
        spec = lax.dot_general(
            syn_ref[:, pl.ds(c * chunk, chunk)],
            back[:, pl.ds(0, (2 + lead) * width)],
            (((0,), (0,)), ((), ())),
            preferred_element_type=F32,
        )
        parts = [
            spec[:, :width] - span_slope(spec[:, width : 2 * width], c * chunk, total)
        ]
        if field == 0:
            parts.append(spec[:, 2 * width :])
        for i, part in enumerate(parts):
            part = part.astype(BF16)
            for b in range(chunk // rows):
                out_ref[c * (chunk // rows) + b, i] = part[b * rows : (b + 1) * rows]


class SlotTables:
    def __init__(self, deg_ref, side_ref, link_ref):
        slots = side_ref.shape[1]
        self.slots = slots
        self.sub = lax.broadcasted_iota(jnp.int32, (slots, slots), 0)
        self.lane = lax.broadcasted_iota(jnp.int32, (slots, slots), 1)
        self.eye = self.sub == self.lane
        side = side_ref[...]
        element = side >> 2
        code = side & 3
        start = jnp.where(code == 0, 0, jnp.where(code == 1, 7, jnp.where(code == 2, 63, 56)))
        step = jnp.where(code == 0, 1, jnp.where(code == 1, 8, jnp.where(code == 2, -1, -8)))
        first = (element >> 1) * LANES + (element & 1) + 2 * start
        self.first_row = first.astype(F32)
        self.step_row = (2 * step).astype(F32)
        self.flip_row = link_ref[0:1, :].astype(F32)
        self.peer_row = link_ref[1:2, :].astype(F32)
        self.slot_row = link_ref[2:3, :].astype(F32)
        element_col = self.column(element.astype(F32))
        code_col = self.column((code & 1).astype(F32))
        count = deg_ref.shape[1]
        member = lax.broadcasted_iota(jnp.int32, (slots, count), 1).astype(F32) == element_col
        degree = jnp.where(
            code_col == 0.0, deg_ref[0:1, :].astype(F32), deg_ref[1:2, :].astype(F32)
        )
        self.degree_col = jnp.sum(jnp.where(member, degree, 0.0), axis=1, keepdims=True)
        self.degree_row = jnp.sum(
            jnp.where(self.eye, self.degree_col, 0.0), axis=0, keepdims=True
        )
        self.peer_col = self.column(self.peer_row)

    def column(self, row):
        return jnp.sum(jnp.where(self.eye, row, 0.0), axis=1, keepdims=True)

    def peer_of(self, offset):
        parts = lax.axis_size("elem")
        return ((lax.axis_index("elem") + offset + parts) % parts).astype(F32)

    def chosen(self, offset, before):
        peer = self.peer_of(offset)
        ahead = jnp.where((self.peer_col == peer) & before, 1.0, 0.0)
        place = jnp.sum(ahead, axis=0, keepdims=True)
        order = lax.broadcasted_iota(jnp.int32, (NEAR, self.slots), 0).astype(F32)
        return jnp.where((self.peer_row == peer) & (place == order), 1.0, 0.0)


def send_traces(tables, u_ref, d_ref, left, packed_ref):
    columns = u_ref.shape[1]
    values = jnp.concatenate([u_ref[...], d_ref[...]], axis=0)
    before = tables.sub < tables.lane
    picks = [tables.chosen(offset, before) for offset in OFFSETS]
    picks_all = jnp.concatenate(picks, axis=0).astype(BF16)
    first_col = tables.column(tables.first_row)
    step_col = tables.column(tables.step_row)
    ids = lax.broadcasted_iota(jnp.int32, (tables.slots, columns), 1)
    nt = (((1,), (1,)), ((), ()))
    for k in range(8):
        wanted = (first_col + step_col * float(k)).astype(jnp.int32)
        hot = jnp.where(ids == wanted, 1.0, 0.0).astype(BF16)
        trace = lax.dot_general(values, hot, nt, preferred_element_type=F32).astype(BF16)
        left[pl.ds(0, LANES), pl.ds(k * 2 * LANES, LANES)] = trace
        packed = lax.dot_general(picks_all, trace, nt, preferred_element_type=F32)
        for o in range(4):
            packed_ref[o, k] = packed[o * NEAR : (o + 1) * NEAR].astype(BF16)
    for o in range(4):
        degree = jnp.sum(picks[o] * tables.degree_row, axis=1, keepdims=True)
        packed_ref[o, 8] = jnp.broadcast_to(degree, (NEAR, LANES)).astype(BF16)


def local_terms(edge_weight, tables, u_ref, d_ref, mass_ref, nears, left, vel_ref, dir_ref):
    rows, columns = u_ref.shape
    slot_col = tables.column(tables.slot_row)

    def aims(match, other_degree):
        def pick(row):
            return jnp.sum(match * row, axis=1, keepdims=True)

        alive = pick(jnp.ones_like(tables.degree_row))
        return alive, pick(tables.first_row), pick(tables.step_row), pick(
            tables.degree_row
        ), other_degree

    mine = tables.peer_of(0)
    match = jnp.where(
        (tables.peer_col == mine) & (slot_col == tables.lane.astype(F32)), 1.0, 0.0
    )
    flips = [tables.column(tables.flip_row)]
    sets = [aims(match, tables.degree_col)]
    before = slot_col < tables.slot_row
    for o, offset in enumerate(OFFSETS):
        match = tables.chosen(offset, before)
        flips.append(jnp.sum(match * tables.flip_row, axis=1, keepdims=True))
        sets.append(aims(match, nears[o, 8].astype(F32)[:, 0:1]))
    filler = 2 * LANES - tables.slots - 4 * NEAR
    zeros = jnp.zeros((filler, 1), F32)

    def joined(parts):
        return jnp.concatenate(list(parts) + [zeros], axis=0)

    alive = joined(s[0] for s in sets)
    first = joined(s[1] for s in sets)
    step = joined(s[2] for s in sets)
    degree = jnp.maximum(joined(s[3] for s in sets), joined(s[4] for s in sets))
    flip = joined(flips)
    first = jnp.where(alive > 0.0, first + 7.0 * flip * step, -1.0e6)
    step = step * (1.0 - 2.0 * flip)
    strength = alive * PENALTY * (degree + 1.0) * (degree + 1.0)
    for k in range(8):
        received = jnp.concatenate(
            [nears[o, k].astype(F32) for o in range(4)] + [jnp.zeros((filler, LANES), F32)],
            axis=0,
        )
        left[pl.ds(0, LANES), pl.ds((k * 2 + 1) * LANES, LANES)] = received.T.astype(BF16)
    left[pl.ds(LANES, 16), :] = jnp.ones((16, left.shape[1]), BF16)
    wide = 256
    ids = lax.broadcasted_iota(jnp.int32, (2 * LANES, wide), 1)
    targets = [(first + step * float(k)).astype(jnp.int32) for k in range(8)]
    factors = [strength * float(edge_weight[k]) for k in range(8)]
    mass = HELM_LAMBDA * jnp.concatenate([mass_ref[...]] * (wide // LANES), axis=1)
    for c in range(columns // wide):
        hot = jnp.concatenate(
            [
                jnp.where(ids == targets[k] - c * wide, factors[k], 0.0).astype(BF16)
                for k in range(8)
            ],
            axis=0,
        )
        summed = jnp.dot(left[...], hot, preferred_element_type=F32)
        scale = mass + summed[LANES : LANES + 1, :]
        span = pl.ds(c * wide, wide)
        vel_ref[:, span] = scale * u_ref[:, span].astype(F32) - summed[:rows]
        dir_ref[:, span] = scale * d_ref[:, span].astype(F32) - summed[rows : 2 * rows]


ROUTES = [(dz, dc) for dz in (4, 3, 5, 2, 6, 1, 7, 0) for dc in (0, 1) if (dz, dc) != (0, 0)]


def whole_kernel(
    edge_weight,
    u_hbm,
    d_hbm,
    adv_hbm,
    visc_hbm,
    syn_hbm,
    fwd_hbm,
    bwd_hbm,
    mass_hbm,
    deg_ref,
    side_ref,
    link_ref,
    got_u,
    got_d,
    local_hbm,
    u_ref,
    d_ref,
    adv_ref,
    visc_ref,
    syn_ref,
    fwd_ref,
    bwd_ref,
    mass_ref,
    local,
    stack,
    back,
    ret_u,
    ret_d,
    left,
    packed,
    nears,
    load_sem,
    in_send,
    in_recv,
    u_send,
    u_recv,
    d_send,
    d_recv,
    halo_send,
    halo_recv,
    relay_in,
    relay_u,
    leg_send,
    leg_recv,
):
    elem = lax.axis_index("elem")
    mode = lax.axis_index("mode")
    parts = lax.axis_size("elem")
    chips = lax.axis_size("mode") // 2
    chip = lax.div(mode, 2)
    core = lax.rem(mode, 2)
    rows = u_ref.shape[0]
    width = visc_ref.shape[1]
    modes_to = [
        lax.rem(chip + dz, chips) * 2 + lax.rem(core + dc, 2) for dz, dc in ROUTES
    ]
    elems_to = [lax.rem(elem + offset + parts, parts) for offset in OFFSETS]
    mesh_ids = pl.DeviceIdType.MESH

    barrier = pltpu.get_barrier_semaphore()
    for other in modes_to:
        pl.semaphore_signal(barrier, inc=1, device_id=(elem, other), device_id_type=mesh_ids)
    for other in elems_to:
        pl.semaphore_signal(barrier, inc=1, device_id=(other, mode), device_id_type=mesh_ids)
    pairs = (
        (u_hbm, u_ref),
        (d_hbm, d_ref),
        (syn_hbm, syn_ref),
        (fwd_hbm, fwd_ref),
        (bwd_hbm, bwd_ref),
        (mass_hbm, mass_ref),
        (visc_hbm, visc_ref),
        (adv_hbm, adv_ref),
    )
    loads = [
        pltpu.make_async_copy(source, target, load_sem.at[i])
        for i, (source, target) in enumerate(pairs)
    ]
    for load in loads:
        load.start()
    pl.semaphore_wait(barrier, len(modes_to) + len(elems_to))

    my_rows = pl.ds(pl.multiple_of(mode * rows, rows), rows)
    up = lax.rem(chip + 2, chips)
    down = lax.rem(chip + chips - 2, chips)
    swapped = lax.rem(core + 1, 2)
    relays = (up * 2 + core, down * 2 + core)
    origins = (down * 2 + core, up * 2 + core)
    onward = (up * 2 + core, down * 2 + swapped)

    def remote(source, target, send, recv, other):
        copy = pltpu.make_async_remote_copy(
            src_ref=source,
            dst_ref=target,
            send_sem=send,
            recv_sem=recv,
            device_id=(elem, other),
            device_id_type=mesh_ids,
        )
        copy.start()
        return copy

    def block_of(index, size):
        return pl.ds(pl.multiple_of(index * size, size), size)

    def send_block(f, source, j):
        other = modes_to[j]
        return remote(
            source.at[:, block_of(other, width)],
            stack.at[f, my_rows, pl.ds(0, width)],
            in_send.at[f, j],
            in_recv.at[f, j],
            other,
        )

    sources = (u_hbm, d_hbm)
    legs = [
        remote(
            sources[f].at[:, block_of(modes_to[t], width)],
            relay_in.at[f, t],
            leg_send.at[f, t],
            leg_recv.at[f, t],
            relays[t],
        )
        for f in range(2)
        for t in range(2)
    ]
    incoming = [[send_block(0, u_hbm, j) for j in range(2, len(ROUTES))], []]
    for leg in legs:
        leg.wait_recv()
    for f in range(2):
        for t in range(2):
            incoming[f].append(
                remote(
                    relay_in.at[f, t],
                    stack.at[f, block_of(origins[t], rows), pl.ds(0, width)],
                    in_send.at[f, t],
                    in_recv.at[f, t],
                    onward[t],
                )
            )
    incoming[1] += [send_block(1, d_hbm, j) for j in range(2, len(ROUTES))]
    tables = SlotTables(deg_ref, side_ref, link_ref)
    for load in loads[:2]:
        load.wait()
    send_traces(tables, u_ref, d_ref, left, packed)
    halo = []
    for o, other in enumerate(elems_to):
        copy = pltpu.make_async_remote_copy(
            src_ref=packed.at[o],
            dst_ref=nears.at[(o + 2) % 4],
            send_sem=halo_send.at[o],
            recv_sem=halo_recv.at[o],
            device_id=(other, mode),
            device_id_type=mesh_ids,
        )
        copy.start()
        halo.append(copy)
    for f, source in enumerate((u_ref, d_ref)):
        stack[f, my_rows, pl.ds(0, width)] = source[
            :, pl.ds(pl.multiple_of(mode * width, width), width)
        ]
    for load in loads[2:]:
        load.wait()
    outgoing = []
    stores = []
    for f, (ret, got, send, recv) in enumerate(
        ((ret_u, got_u, u_send, u_recv), (ret_d, got_d, d_send, d_recv))
    ):
        for copy in incoming[f]:
            copy.wait_recv()
        field_planes(
            f, adv_ref, visc_ref, syn_ref, fwd_ref, bwd_ref, mass_ref, stack, back, ret
        )
        copies = []
        if f == 0:
            legs_u = [
                remote(
                    ret.at[modes_to[t]], relay_u.at[t], leg_send.at[2, t], leg_recv.at[2, t],
                    relays[t],
                )
                for t in range(2)
            ]
        else:
            for t in range(2):
                legs_u[t].wait_recv()
                outgoing[0].append(
                    remote(
                        relay_u.at[t], got_u.at[origins[t]], u_send.at[t], u_recv.at[t],
                        onward[t],
                    )
                )
        for j in range(2 if f == 0 else 0, len(ROUTES)):
            other = modes_to[j]
            copies.append(remote(ret.at[other], got.at[mode], send.at[j], recv.at[j], other))
        store = pltpu.make_async_copy(ret.at[mode], got.at[mode], load_sem.at[8 + f])
        store.start()
        stores.append(store)
        outgoing.append(copies)
    for copy in halo:
        copy.wait_recv()
    local_terms(
        edge_weight, tables, u_ref, d_ref, mass_ref, nears, left, local.at[0], local.at[1]
    )
    store = pltpu.make_async_copy(local, local_hbm, load_sem.at[10])
    store.start()
    stores.append(store)
    for copy in outgoing[0] + outgoing[1]:
        copy.wait_recv()
    for store in stores:
        store.wait()
    for copy in incoming[0] + incoming[1] + halo + outgoing[0] + outgoing[1] + legs + legs_u:
        copy.wait_send()


def final_kernel(got_u, got_d, local, adv_out, vel_out, dir_out):
    width = got_u.shape[3]
    for b in range(got_u.shape[0]):
        span = pl.ds(b * width, width)
        vel_out[:, span] = local[0, :, span] + got_u[b, 0].astype(F32)
        adv_out[:, span] = got_u[b, 1].astype(F32)
        dir_out[:, span] = local[1, :, span] + got_d[b, 0].astype(F32)


VMEM_BYTES = 67043328


def on_device(u_spec, dir_spec, advecting, viscosity, degrees, edge_side, edge_link):
    modes = lax.axis_size("mode")
    total, width = viscosity.shape
    rows, columns = u_spec.shape
    forward, backward, mass = operator_tables(degrees.shape[1] // modes)
    weights = LENGTH * cheb_tables()[1]
    shape = jax.ShapeDtypeStruct
    near = pl.BlockSpec(memory_space=pltpu.VMEM)
    far = pl.BlockSpec(memory_space=pltpu.HBM)
    routes = len(ROUTES)
    got_u, got_d, local = pl.pallas_call(
        lambda *refs: whole_kernel(weights, *refs),
        out_shape=(
            shape((modes, 2, rows, width), BF16),
            shape((modes, 1, rows, width), BF16),
            shape((2, rows, columns), F32),
        ),
        in_specs=[far] * 8 + [near] * 3,
        out_specs=(far, far, far),
        scratch_shapes=[
            pltpu.VMEM((rows, columns), BF16),
            pltpu.VMEM((rows, columns), BF16),
            pltpu.VMEM((3, total, width), BF16),
            pltpu.VMEM((total, width), BF16),
            pltpu.VMEM((total, total), BF16),
            pltpu.VMEM(forward.shape, BF16),
            pltpu.VMEM(backward.shape, BF16),
            pltpu.VMEM(mass.shape, F32),
            pltpu.VMEM((2, rows, columns), F32),
            pltpu.VMEM((2, total, 2 * width), BF16),
            pltpu.VMEM((total, 3 * width), BF16),
            pltpu.VMEM((modes, 2, rows, width), BF16),
            pltpu.VMEM((modes, 1, rows, width), BF16),
            pltpu.VMEM((LANES + 16, 16 * LANES), BF16),
            pltpu.VMEM((4, 9, NEAR, LANES), BF16),
            pltpu.VMEM((4, 9, NEAR, LANES), BF16),
            pltpu.SemaphoreType.DMA((11,)),
            pltpu.SemaphoreType.DMA((2, routes)),
            pltpu.SemaphoreType.DMA((2, routes)),
            pltpu.SemaphoreType.DMA((routes,)),
            pltpu.SemaphoreType.DMA((routes,)),
            pltpu.SemaphoreType.DMA((routes,)),
            pltpu.SemaphoreType.DMA((routes,)),
            pltpu.SemaphoreType.DMA((4,)),
            pltpu.SemaphoreType.DMA((4,)),
            pltpu.VMEM((2, 2, rows, width), BF16),
            pltpu.VMEM((2, 2, rows, width), BF16),
            pltpu.SemaphoreType.DMA((3, 2)),
            pltpu.SemaphoreType.DMA((3, 2)),
        ],
        name="whole",
        compiler_params=pltpu.CompilerParams(
            collective_id=0, has_side_effects=True, vmem_limit_bytes=VMEM_BYTES
        ),
    )(
        u_spec,
        dir_spec,
        advecting,
        viscosity,
        synthesis_table(total),
        forward,
        backward,
        mass,
        degrees,
        edge_side[None, :],
        edge_link,
    )
    out = shape((rows, columns), F32)
    return pl.pallas_call(
        final_kernel,
        out_shape=(out, out, out),
        name="final",
        compiler_params=pltpu.CompilerParams(vmem_limit_bytes=VMEM_BYTES),
    )(got_u, got_d, local)


def solution(mesh):
    in_specs = (
        P("mode", "elem"),
        P("mode", "elem"),
        P(None, None, ("elem", "mode")),
        P(None, ("elem", "mode")),
        P(None, "elem"),
        P("elem"),
        P(None, "elem"),
    )
    out_specs = (P("mode", "elem"), P("mode", "elem"), P("mode", "elem"))
    return jax.shard_map(
        on_device, mesh=mesh, in_specs=in_specs, out_specs=out_specs, check_vma=False
    )
```
